32 devices in a mesh: dp: 8 (over z, y), shard: 4 (over x, core).
Axes of the slice: x: 2, y: 2, z: 4, core: 2. Of those that a mesh axis runs over, the one named last changes fastest.
Arguments:
- tokens: bfloat16 [8, 2048, 1024], P('dp', 'shard'), may hold values from -6 to 6
- segments: int32 [8, 2048], P('dp', 'shard'), may hold values from 0 to 3, never falling along the last dimension, each value on 1 to 1024 neighbouring positions
- cotangent: bfloat16 [8, 2048, 1024], P('dp', 'shard'), may hold values from -6 to 6
- query_weight: float32 [1024, 256], P(('dp', 'shard')), may hold values from -0.1875 to 0.1875
- key_weight: float32 [1024, 256], P(('dp', 'shard')), may hold values from -0.1875 to 0.1875
- value_weight: float32 [1024, 1024], P(('dp', 'shard')), may hold values from -0.1875 to 0.1875
- output_weight: float32 [1024, 1024], P(('dp', 'shard')), may hold values from -3 to 3
- gate_weight: float32 [1024, 2752], P(('dp', 'shard')), may hold values from -0.1875 to 0.1875
- up_weight: float32 [1024, 2752], P(('dp', 'shard')), may hold values from -0.1875 to 0.1875
- down_weight: float32 [1024, 2752], P(('dp', 'shard')), may hold values from -0.109375 to 0.109375
- norm_gains: float32 [2, 1024], P(None, ('dp', 'shard')), may hold values from 0.5 to 1.5
- query_first: float32 [1024, 256], P(('dp', 'shard')), may hold values from -2 to 2
- key_first: float32 [1024, 256], P(('dp', 'shard')), may hold values from -2 to 2
- value_first: float32 [1024, 1024], P(('dp', 'shard')), may hold values from -1 to 1
- output_first: float32 [1024, 1024], P(('dp', 'shard')), may hold values from -0.0625 to 0.0625
- gate_first: float32 [1024, 2752], P(('dp', 'shard')), may hold values from -0.25 to 0.25
- up_first: float32 [1024, 2752], P(('dp', 'shard')), may hold values from -0.25 to 0.25
- down_first: float32 [1024, 2752], P(('dp', 'shard')), may hold values from -0.4375 to 0.4375
- gains_first: float32 [2, 1024], P(None, ('dp', 'shard')), may hold values from -1.25 to 1.25
- query_second: float32 [1024, 256], P(('dp', 'shard')), may hold values from 0.00578 to 0.09248
- key_second: float32 [1024, 256], P(('dp', 'shard')), may hold values from 0.00578 to 0.09248
- value_second: float32 [1024, 1024], P(('dp', 'shard')), may hold values from 0.001445 to 0.02312
- output_second: float32 [1024, 1024], P(('dp', 'shard')), may hold values from 5e-06 to 8e-05
- gate_second: float32 [1024, 2752], P(('dp', 'shard')), may hold values from 8.405e-05 to 0.0013448
- up_second: float32 [1024, 2752], P(('dp', 'shard')), may hold values from 8.405e-05 to 0.0013448
- down_second: float32 [1024, 2752], P(('dp', 'shard')), may hold values from 0.00022445 to 0.0035912
- gains_second: float32 [2, 1024], P(None, ('dp', 'shard')), may hold values from 0.002 to 0.032
Outputs:
- block_out: bfloat16 [8, 2048, 1024], P('dp', 'shard')
- input_grad: float32 [8, 2048, 1024], P('dp', 'shard')
- grad_norm: float32 [1], replicated
- query_master: float32 [1024, 256], P(('dp', 'shard'))
- key_master: float32 [1024, 256], P(('dp', 'shard'))
- value_master: float32 [1024, 1024], P(('dp', 'shard'))
- output_master: float32 [1024, 1024], P(('dp', 'shard'))
- gate_master: float32 [1024, 2752], P(('dp', 'shard'))
- up_master: float32 [1024, 2752], P(('dp', 'shard'))
- down_master: float32 [1024, 2752], P(('dp', 'shard'))
- gains_master: float32 [2, 1024], P(None, ('dp', 'shard'))
- query_momentum: float32 [1024, 256], P(('dp', 'shard'))
- key_momentum: float32 [1024, 256], P(('dp', 'shard'))
- value_momentum: float32 [1024, 1024], P(('dp', 'shard'))
- output_momentum: float32 [1024, 1024], P(('dp', 'shard'))
- gate_momentum: float32 [1024, 2752], P(('dp', 'shard'))
- up_momentum: float32 [1024, 2752], P(('dp', 'shard'))
- down_momentum: float32 [1024, 2752], P(('dp', 'shard'))
- gains_momentum: float32 [2, 1024], P(None, ('dp', 'shard'))
- query_variance: float32 [1024, 256], P(('dp', 'shard'))
- key_variance: float32 [1024, 256], P(('dp', 'shard'))
- value_variance: float32 [1024, 1024], P(('dp', 'shard'))
- output_variance: float32 [1024, 1024], P(('dp', 'shard'))
- gate_variance: float32 [1024, 2752], P(('dp', 'shard'))
- up_variance: float32 [1024, 2752], P(('dp', 'shard'))
- down_variance: float32 [1024, 2752], P(('dp', 'shard'))
- gains_variance: float32 [2, 1024], P(None, ('dp', 'shard'))
The draws below stay inside these ranges and needn't reach their ends.
Inputs may be any that keep to these rules, and one draw needn't show every extreme that they name: `segments`: in each row the ids never fall and each of 0 to 3 appears; a document has 1 to 1024 positions, and some document has exactly 1024.
All inputs are finite; a program needn't handle non-finite values.
Results may differ from the reference program's by a relative error of at most 0.0091.
The reference program's roundings to bfloat16 on the way count: a program that leaves them out, or rounds other values in their place, can miss the bound.
Values may be sent and summed in bfloat16 or wider, within the bound.
No kernel may reach another device: no remote copies, remote signals or barrier semaphores. Data moves between devices by JAX's collectives and lax.ppermute only.
A program may use at most 256 MiB of HBM per device.

```python
import math
import jax
import jax.numpy as jnp
import numpy as np
from jax import lax

D = 1024
FH = 16
FD = 16
VD = 64
FF = 2752
SEQ = 2048
DOCS = 4
STEP = 10
ROW_DEV = 1
QW = 256
VW = 1024
FEAT = 273
ROWS = 8
NPARAMS = 11077632
N_SHARD = 4


def spiked(drawn, own_key, source, target, parts, factor):
    owner, partner = [(jnp.arange(drawn.shape[position]) // (drawn.shape[position] // parts)).reshape([-1 if axis == position else 1 for axis in range(drawn.ndim)]) for position in (source, target)]
    chosen = jax.random.permutation(own_key, parts)[partner]
    strong = (owner == chosen) | (owner == (partner + parts // 2) % parts)
    return jnp.where(strong, factor * drawn, drawn)


def block_scale(stream_key, dims, cuts, least, largest):
    loudness = 1.0
    for position, shards_of in cuts:
        heights = jax.random.uniform(jax.random.fold_in(jax.random.fold_in(stream_key, 6), position), (shards_of,), jnp.float32, least / len(cuts), largest / len(cuts))
        loudness = loudness * jnp.repeat(jnp.exp(heights), dims[position] // shards_of).reshape((-1,) + (1,) * (len(dims) - 1 - position))
    return loudness


def profile(number_of, total, most, lean):
    weights = [(1 << 20) // math.isqrt(rank ** lean) + 1 for rank in range(2, number_of + 1)]
    spare, given = total - most - (number_of - 1), [1] * (number_of - 1)
    while spare > 0:
        movable = [i for i in range(number_of - 1) if given[i] < most]
        mass, budget = sum([weights[i] for i in movable]), spare
        for i in movable:
            more = min(most - given[i], max(1, budget * weights[i] // mass), spare)
            given[i] = given[i] + more
            spare = spare - more
    return np.array([most] + given)


def uneven_parts(rng, number_of, total, bound, slope):
    if number_of == 2:
        one = jax.random.randint(rng, (), max(1, total - bound), min(bound, total - 1) + 1)
        return jnp.stack([one, total - one])
    tallies = jnp.asarray(profile(number_of, total, bound, slope), jnp.int32)
    couples = (number_of - 1) // 2
    donor, receiver = tallies[1:1 + 2 * couples:2], tallies[2:2 + 2 * couples:2]
    room = jnp.minimum(donor - 1, bound - receiver)
    shifted = jax.random.randint(jax.random.fold_in(rng, 1), (couples,), 0, 1 << 20) % (room + 1)
    tallies = tallies.at[1:1 + 2 * couples:2].set(donor - shifted).at[2:2 + 2 * couples:2].set(receiver + shifted)
    return tallies[jax.random.permutation(jax.random.fold_in(rng, 2), number_of)]


def gaussian(own_key, dims, deviation, reach, shards=(), held_as=jnp.bfloat16):
    array = jax.random.normal(own_key, dims, jnp.float32) * deviation
    if len(shards) > 0:
        array = block_scale(own_key, dims, shards, -0.22, 0.18) * array
    return jnp.clip(array, min=-reach, max=reach).astype(held_as)


def bell_draw_with(stream_key, dims, scale, most, cuts, heavy, held_as=jnp.bfloat16):
    entries = scale * jax.random.normal(stream_key, dims, jnp.float32)
    if cuts:
        entries = entries * block_scale(stream_key, dims, cuts, -0.22, 0.18)
    return jnp.clip(spiked(entries, jax.random.fold_in(stream_key, 3), *heavy), -most, most).astype(held_as)


def setup_inputs(seed: int = 0) -> dict:
    keys = jax.random.split(jax.random.key(seed), 28)
    return {
        "tokens": gaussian(keys[0], (ROWS, SEQ, D), 1.0, 6.0, ((0, 8), (1, 4))),
        "segments": jax.vmap(lambda own: jnp.searchsorted(jnp.cumsum(uneven_parts(own, DOCS, SEQ, SEQ // 2, 1)), jnp.arange(SEQ), side="right"))(jax.random.split(keys[1], ROWS)).reshape((ROWS, SEQ)).astype(jnp.int32),
        "cotangent": bell_draw_with(keys[2], (ROWS, SEQ, D), 1.0, 6.0, ((0, 8), (1, 4)), (0, 2, 8, 2.0)),
        "query_weight": gaussian(keys[3], (D, QW), D ** -0.5, 0.1875, ((0, 32),), jnp.float32),
        "key_weight": gaussian(keys[4], (D, QW), D ** -0.5, 0.1875, ((0, 32),), jnp.float32),
        "value_weight": gaussian(keys[5], (D, VW), D ** -0.5, 0.1875, ((0, 32),), jnp.float32),
        "output_weight": gaussian(keys[6], (D, VW), (max(D // 256, 1)) ** -0.5, 3.0, ((0, 32),), jnp.float32),
        "gate_weight": gaussian(keys[7], (D, FF), D ** -0.5, 0.1875, ((0, 32),), jnp.float32),
        "up_weight": gaussian(keys[8], (D, FF), D ** -0.5, 0.1875, ((0, 32),), jnp.float32),
        "down_weight": gaussian(keys[9], (D, FF), FF ** -0.5, 0.109375, ((0, 32),), jnp.float32),
        "norm_gains": jnp.clip(1.0 + 0.1 * jax.random.normal(keys[10], (2, D), jnp.float32), 0.5, 1.5),
        "query_first": gaussian(keys[11], (D, QW), (0.11 * 3.4), 2.0, ((0, 32),), jnp.float32),
        "key_first": gaussian(keys[12], (D, QW), (0.11 * 3.4), 2.0, ((0, 32),), jnp.float32),
        "value_first": gaussian(keys[13], (D, VW), (0.11 * 1.7), 1.0, ((0, 32),), jnp.float32),
        "output_first": gaussian(keys[14], (D, VW), (0.11 * 0.1), 0.0625, ((0, 32),), jnp.float32),
        "gate_first": gaussian(keys[15], (D, FF), (0.11 * 0.41), 0.25, ((0, 32),), jnp.float32),
        "up_first": gaussian(keys[16], (D, FF), (0.11 * 0.41), 0.25, ((0, 32),), jnp.float32),
        "down_first": gaussian(keys[17], (D, FF), (0.11 * 0.67), 0.4375, ((0, 32),), jnp.float32),
        "gains_first": gaussian(keys[18], (2, D), (0.11 * 2.0), 1.25, ((1, 32),), jnp.float32),
        "query_second": jnp.clip(jnp.exp(math.log(0.09248) - 2.7725887 * jax.random.uniform(keys[19], (D, QW), jnp.float32) ** block_scale(keys[19], (D, QW), ((0, 32),), -0.2, 0.2)), 0.00578, 0.09248),
        "key_second": jnp.clip(jnp.exp(math.log(0.09248) - 2.7725887 * jax.random.uniform(keys[20], (D, QW), jnp.float32) ** block_scale(keys[20], (D, QW), ((0, 32),), -0.2, 0.2)), 0.00578, 0.09248),
        "value_second": jnp.clip(jnp.exp(math.log(0.02312) - 2.7725887 * jax.random.uniform(keys[21], (D, VW), jnp.float32) ** block_scale(keys[21], (D, VW), ((0, 32),), -0.2, 0.2)), 0.001445, 0.02312),
        "output_second": jnp.clip(jnp.exp(math.log(7.999999797903001e-05) - 2.7725887 * jax.random.uniform(keys[22], (D, VW), jnp.float32) ** block_scale(keys[22], (D, VW), ((0, 32),), -0.2, 0.2)), 4.999999873689376e-06, 7.999999797903001e-05),
        "gate_second": jnp.clip(jnp.exp(math.log(0.0013448) - 2.7725887 * jax.random.uniform(keys[23], (D, FF), jnp.float32) ** block_scale(keys[23], (D, FF), ((0, 32),), -0.2, 0.2)), 8.40499997138977e-05, 0.0013448),
        "up_second": jnp.clip(jnp.exp(math.log(0.0013448) - 2.7725887 * jax.random.uniform(keys[24], (D, FF), jnp.float32) ** block_scale(keys[24], (D, FF), ((0, 32),), -0.2, 0.2)), 8.40499997138977e-05, 0.0013448),
        "down_second": jnp.clip(jnp.exp(math.log(0.0035912) - 2.7725887 * jax.random.uniform(keys[25], (D, FF), jnp.float32) ** block_scale(keys[25], (D, FF), ((0, 32),), -0.2, 0.2)), 0.00022445, 0.0035912),
        "gains_second": jnp.clip(jnp.exp(math.log(0.032) - 2.7725887 * jax.random.uniform(keys[26], (2, D), jnp.float32) ** block_scale(keys[26], (2, D), ((1, 32),), -0.2, 0.2)), 0.002, 0.032),
    }


@jax.custom_vjp
def low(v):
    return lax.optimization_barrier(v.astype(jnp.bfloat16)).astype(jnp.float32)

@jax.custom_vjp
def low_back(v):
    return v

def low_keep(v):
    return (low(v), None)

def low_pass(kept, grad):
    return (grad,)

def back_keep(v):
    return (v, None)

def back_low(kept, grad):
    return (low(grad),)
low.defvjp(low_keep, low_pass)
low_back.defvjp(back_keep, back_low)
EPS_NORM = 1e-05
BETA_ONE = 0.9
BETA_TWO = 0.999
ADAM_EPS = 1e-08
HIGHEST_MODE = lax.Precision.HIGHEST

def rms_scale(value, gain):
    return value * lax.rsqrt(lax.optimization_barrier(jnp.mean(value * value, axis=-1, keepdims=True)) + EPS_NORM) * gain

def features(vector, fdim):
    lead = vector.shape[:-1]
    outer = (vector[..., :, None] * vector[..., None, :]).reshape(lead + (fdim * fdim,))
    ones = jnp.ones(lead + (1,), jnp.float32)
    return jnp.concatenate([ones, vector * fdim ** (-0.25), outer * (2.0 * fdim) ** (-0.5)], axis=-1)

def block_mix(query, key, value, seg, state, norm_state, last):
    fdim = query.shape[-1]
    inner = jnp.einsum('thf,shf->hts', query, key, precision=HIGHEST_MODE) * fdim ** (-0.5)
    kernel = 1.0 + inner + 0.5 * inner * inner
    place = jnp.arange(query.shape[0])
    visible = (place[None, :] <= place[:, None]) & (seg[None, :] == seg[:, None])
    kernel = jnp.where(visible[None], kernel, 0.0)
    numer = jnp.einsum('hts,shv->thv', kernel, value, precision=HIGHEST_MODE)
    denom = jnp.transpose(lax.optimization_barrier(jnp.sum(kernel, axis=2)))
    q_feat = features(query, fdim)
    carried = (seg == last).astype(jnp.float32)[:, None]
    numer = numer + carried[:, :, None] * jnp.einsum('thp,hpv->thv', q_feat, state, precision=HIGHEST_MODE)
    denom = denom + carried * jnp.einsum('thp,hp->th', q_feat, norm_state, precision=HIGHEST_MODE)
    return numer / denom[:, :, None]

def block_state(key, value, seg):
    fdim = key.shape[-1]
    chosen = (seg == seg[-1]).astype(jnp.float32)[:, None, None]
    k_feat = features(key, fdim) * chosen
    return (jnp.einsum('thp,thv->hpv', k_feat, value, precision=HIGHEST_MODE), lax.optimization_barrier(jnp.sum(k_feat, axis=0)))

def row_mix(query, key, value, seg):
    blocks = N_SHARD
    size = query.shape[0] // blocks
    pieces = (query.reshape(blocks, size, FH, FD), key.reshape(blocks, size, FH, FD), value.reshape(blocks, size, FH, VD), seg.reshape(blocks, size))

    def advance(carry, piece):
        state, norm_state, last = carry
        q_block, k_block, v_block, s_block = piece
        out = block_mix(q_block, k_block, v_block, s_block, state, norm_state, last)
        new_state, new_norm = block_state(k_block, v_block, s_block)
        keep = (last == s_block[-1]).astype(jnp.float32)
        return ((new_state + keep * state, new_norm + keep * norm_state, s_block[-1]), out)
    start = (jnp.zeros((FH, FEAT, VD), jnp.float32), jnp.zeros((FH, FEAT), jnp.float32), jnp.float32(-1.0))
    _, outs = lax.scan(jax.checkpoint(advance), start, pieces)
    return outs.reshape(query.shape[0], FH, VD)

def forward(x, w_query, w_key, w_value, w_output, w_gate, w_up, w_down, gains, seg):
    rows, length, width = x.shape
    normed_one = low(rms_scale(x, gains[0]))
    query = low_back(low(jnp.einsum('rtd,de->rte', normed_one, w_query, precision=HIGHEST_MODE)))
    key = low_back(low(jnp.einsum('rtd,de->rte', normed_one, w_key, precision=HIGHEST_MODE)))
    value = low_back(low(jnp.einsum('rtd,de->rte', normed_one, w_value, precision=HIGHEST_MODE)))
    mixed = jax.vmap(row_mix)(query.reshape(rows, length, FH, FD), key.reshape(rows, length, FH, FD), value.reshape(rows, length, FH, VD), seg)
    mixed = low(mixed.reshape(rows, length, FH * VD))
    branch = low_back(jnp.einsum('rte,de->rtd', mixed, w_output, precision=HIGHEST_MODE))
    hidden = x + branch
    normed_two = low(rms_scale(hidden, gains[1]))
    gate = low_back(jnp.einsum('rtd,df->rtf', normed_two, w_gate, precision=HIGHEST_MODE))
    lift = low_back(jnp.einsum('rtd,df->rtf', normed_two, w_up, precision=HIGHEST_MODE))
    act = low(jax.nn.silu(gate) * lift)
    return hidden + jnp.einsum('rtf,df->rtd', act, w_down, precision=HIGHEST_MODE)

def adam_step(weight, first, second, grad, rate, decay, count):
    momentum = BETA_ONE * first + (1.0 - BETA_ONE) * grad
    variance = BETA_TWO * second + (1.0 - BETA_TWO) * grad * grad
    mean_hat = momentum / (1.0 - BETA_ONE ** count)
    var_hat = variance / (1.0 - BETA_TWO ** count)
    master = weight - rate * (mean_hat / (jnp.sqrt(var_hat) + ADAM_EPS) + decay * weight)
    return (master, momentum, variance)

def reference(tokens, segments, cotangent, query_weight, key_weight, value_weight, output_weight, gate_weight, up_weight, down_weight, norm_gains, query_first, key_first, value_first, output_first, gate_first, up_first, down_first, gains_first, query_second, key_second, value_second, output_second, gate_second, up_second, down_second, gains_second):
    masters = (query_weight, key_weight, value_weight, output_weight, gate_weight, up_weight, down_weight, norm_gains)
    firsts = (query_first, key_first, value_first, output_first, gate_first, up_first, down_first, gains_first)
    seconds = (query_second, key_second, value_second, output_second, gate_second, up_second, down_second, gains_second)
    weights = tuple((low(w) for w in masters))
    groups = ROWS // ROW_DEV
    inputs = tokens.astype(jnp.float32).reshape(groups, ROW_DEV, SEQ, D)
    segs = segments.astype(jnp.float32).reshape(groups, ROW_DEV, SEQ)
    backs = cotangent.astype(jnp.float32).reshape(groups, ROW_DEV, SEQ, D)

    def group(total, piece):
        x_part, s_part, c_part = piece

        def apply(xx, wq, wk, wv, wo, wg, wu, wd, gg):
            return forward(xx, wq, wk, wv, wo, wg, wu, wd, gg, s_part)
        out, pull = jax.vjp(apply, x_part, weights[0], weights[1], weights[2], weights[3], weights[4], weights[5], weights[6], weights[7])
        grads = pull(c_part)
        return (tuple((a + b for a, b in zip(total, grads[1:]))), (out.astype(jnp.bfloat16), grads[0]))
    zeros = tuple((jnp.zeros_like(w) for w in weights))
    totals, (outs, input_grads) = lax.scan(group, zeros, (inputs, segs, backs))
    squares = jnp.float32(0.0)
    for grad in totals:
        squares = squares + jnp.sum(grad * grad)
    grad_norm = jnp.sqrt(squares)
    factor = jnp.minimum(1.0, math.sqrt(NPARAMS) / (grad_norm + 1e-06))
    count = float(STEP)
    rates = (D ** (-0.5), D ** (-0.5), D ** (-0.5), max(D // 256, 1) ** (-0.5), D ** (-0.5), D ** (-0.5), FF ** (-0.5), 0.3)
    decays = (0.1, 0.1, 0.1, 0.1, 0.1, 0.1, 0.1, 0.0)
    new_masters, new_firsts, new_seconds = ([], [], [])
    for index in range(8):
        master, momentum, variance = adam_step(masters[index], firsts[index], seconds[index], totals[index] * factor, rates[index], decays[index], count)
        new_masters.append(master)
        new_firsts.append(momentum)
        new_seconds.append(variance)
    return (outs.reshape(ROWS, SEQ, D), input_grads.reshape(ROWS, SEQ, D), grad_norm.reshape(1), new_masters[0], new_masters[1], new_masters[2], new_masters[3], new_masters[4], new_masters[5], new_masters[6], new_masters[7], new_firsts[0], new_firsts[1], new_firsts[2], new_firsts[3], new_firsts[4], new_firsts[5], new_firsts[6], new_firsts[7], new_seconds[0], new_seconds[1], new_seconds[2], new_seconds[3], new_seconds[4], new_seconds[5], new_seconds[6], new_seconds[7])
```

```python
import math

import jax
import jax.numpy as jnp
import numpy as np
from jax import lax
from jax.experimental import pallas as pl
from jax.experimental.pallas import tpu as pltpu
from jax.sharding import PartitionSpec as P

FH = 16
FD = 16
VD = 64
STEP = 10
NPARAMS = 11077632
DOC_MAX = 1024
BOTH = ("dp", "shard")

EPS_NORM = 1e-05
BETA_ONE = 0.9
BETA_TWO = 0.999
ADAM_EPS = 1e-08

HEAD_PAIRS = FH // 2
TAYLOR = [(i, j) for i in range(FD + 1) for j in range(i, FD + 1)]
NFEAT = 160
WIDE = 256


def feature_table():
    table = np.zeros((8, WIDE), np.int32)
    table[:2] = -1
    for column, (i, j) in enumerate(TAYLOR):
        table[0, column], table[1, column] = i, j
        table[2, column] = 1 if i == j and i < FD else 2
    return table


def nt(left, right):
    return lax.dot_general(
        left, right, (((1,), (1,)), ((), ())), preferred_element_type=jnp.float32
    )


def nn(left, right):
    return lax.dot_general(
        left, right, (((1,), (0,)), ((), ())), preferred_element_type=jnp.float32
    )


def tn(left, right):
    return lax.dot_general(
        left, right, (((0,), (0,)), ((), ())), preferred_element_type=jnp.float32
    )


def lanes_of(shape):
    return lax.broadcasted_iota(jnp.int32, shape, 1)


def pick(table, head, weighted):
    rows = lax.broadcasted_iota(jnp.int32, (WIDE, WIDE), 0) - FD * head
    first, second = table[0:1], table[1:2]
    size = 0.5 * table[2:3].astype(jnp.float32) if weighted else jnp.ones((1, WIDE), jnp.float32)
    inside = (rows >= 0) & (rows < FD)
    one = jnp.where(inside & (rows == first), size, 0.0).astype(jnp.bfloat16)
    two = jnp.where(inside & (rows == second), 1.0, 0.0).astype(jnp.bfloat16)
    flat_one = jnp.where(first == FD, size, 0.0)
    flat_two = jnp.where(second == FD, 1.0, 0.0)
    return one, two, flat_one, flat_two


def factors(vector, chosen):
    one, two, flat_one, flat_two = chosen
    return nn(vector, one) + flat_one, nn(vector, two) + flat_two


def padded(block):
    return jnp.concatenate([block, jnp.zeros((WIDE - block.shape[0], block.shape[1]), block.dtype)], 0)


def state_kernel(k_ref, v_ref, chosen_ref, table_ref, state_ref, den_ref):
    pair = pl.program_id(0)
    table = table_ref[...]
    key = k_ref[...]
    length = key.shape[0]
    wide_v = jnp.concatenate([v_ref[...], jnp.ones((length, 128), jnp.bfloat16)], 1)

    @pl.when(pair == 0)
    def _():
        den_ref[...] = jnp.zeros_like(den_ref)

    lane = lanes_of((NFEAT, 128))
    parts = []
    dens = jnp.zeros((NFEAT, 128), jnp.float32)
    for half in range(2):
        head = 2 * pair + half
        left, right = factors(key, pick(table, head, False))
        feat = (left * right * chosen_ref[...]).astype(jnp.bfloat16)
        both = tn(feat, wide_v)[:NFEAT]
        parts.append(both[:, :128])
        dens = dens + jnp.where(lane == head, both[:, 128:], 0.0)
    state_ref[...] = jnp.where(lane < VD, parts[0], parts[1]).astype(jnp.bfloat16)
    den_ref[...] += dens.astype(jnp.bfloat16)


def head_state(state, den, head):
    lane = lanes_of(den.shape)
    column = jnp.sum(jnp.where(lane == head, den.astype(jnp.float32), 0.0), axis=1, keepdims=True)
    column = jnp.broadcast_to(column, den.shape).astype(jnp.bfloat16)
    return padded(jnp.concatenate([state, column], 1))


def visible_block(seg_col, seg_row, top, rows, cols):
    place = lax.broadcasted_iota(jnp.int32, (rows, cols), 0) + top
    source = lax.broadcasted_iota(jnp.int32, (rows, cols), 1)
    return (source <= place) & (seg_col[top : top + rows] == seg_row[:, :cols])


def mix_kernel(
    q_ref, k_ref, v_ref, segc_ref, segr_ref, carried_ref, state_ref, den_ref, table_ref,
    low_ref, att_ref, norm_ref,
):
    pair = pl.program_id(0)
    table = table_ref[...]
    query, key = q_ref[...], k_ref[...]
    length = key.shape[0]
    block = length // 2
    wide_v = jnp.concatenate([v_ref[...], jnp.ones((length, 128), jnp.bfloat16)], 1)
    state, den = state_ref[...], den_ref[...]
    lane = lanes_of((length, WIDE)) // FD
    atts, norms = [], []
    masks = [
        visible_block(segc_ref[...], segr_ref[...], b * block, block, (b + 1) * block)
        for b in range(2)
    ]
    for half in range(2):
        head = 2 * pair + half
        q_head = jnp.where(lane == head, query, jnp.zeros_like(query))
        left, right = factors(query, pick(table, head, True))
        feat = (left * right * carried_ref[...]).astype(jnp.bfloat16)
        carried = nn(feat, head_state(state, den, head))
        sums = []
        for b in range(2):
            top, end = b * block, (b + 1) * block
            shifted = nt(q_head[top:end], key[:end]) + 1.0
            kernel = jnp.where(masks[b], 0.5 * shifted * shifted + 0.5, 0.0)
            sums.append(nn(kernel.astype(jnp.bfloat16), wide_v[:end]))
        both = jnp.concatenate(sums, 0) + carried
        atts.append(both[:, :128] / both[:, 128:])
        norms.append(both[:, 128:])
    side = lanes_of((length, 128)) < VD
    att = jnp.where(side, atts[0], atts[1])
    low_ref[...] = att.astype(jnp.bfloat16)
    att_ref[...] = att
    norm_ref[...] = jnp.where(side, norms[0], norms[1])


def mix_back_kernel(
    q_ref, k_ref, v_ref, segc_ref, segr_ref, carried_ref, state_ref, den_ref, table_ref,
    att_ref, norm_ref, dm_ref,
    dq_ref, dk_ref, dv_ref, dstate_ref, dden_ref,
):
    pair = pl.program_id(0)
    table = table_ref[...]
    query, key = q_ref[...], k_ref[...]
    length = key.shape[0]
    block = length // 2
    wide_v = jnp.concatenate([v_ref[...], jnp.ones((length, 128), jnp.bfloat16)], 1)
    state, den = state_ref[...], den_ref[...]
    lane = lanes_of((length, WIDE)) // FD
    narrow = lanes_of((length, 128))
    d_num = dm_ref[...] / norm_ref[...]
    weighted = d_num * att_ref[...]

    @pl.when(pair == 0)
    def _():
        dq_ref[...] = jnp.zeros_like(dq_ref)
        dk_ref[...] = jnp.zeros_like(dk_ref)
        dden_ref[...] = jnp.zeros_like(dden_ref)

    masks = [
        visible_block(segc_ref[...], segr_ref[...], b * block, block, (b + 1) * block)
        for b in range(2)
    ]
    flane = lanes_of((NFEAT, 128))
    d_state = jnp.zeros((NFEAT, 128), jnp.float32)
    d_den = jnp.zeros((NFEAT, 128), jnp.float32)
    dv = [jnp.zeros((block, 128), jnp.float32) for _ in range(2)]
    dk = [jnp.zeros((block, WIDE), jnp.float32) for _ in range(2)]
    dq = jnp.zeros((length, WIDE), jnp.float32)
    for half in range(2):
        head = 2 * pair + half
        side = (narrow >= VD) if half else (narrow < VD)
        q_head = jnp.where(lane == head, query, jnp.zeros_like(query))
        k_head = jnp.where(lane == head, key, jnp.zeros_like(key))
        d_bot = -jnp.sum(jnp.where(side, weighted, 0.0), axis=1, keepdims=True)
        high = d_bot.astype(jnp.bfloat16).astype(jnp.float32)
        tail = jnp.where(narrow == 0, high, jnp.where(narrow == 1, d_bot - high, 0.0))
        top_half = jnp.where(side, d_num, 0.0).astype(jnp.bfloat16)
        wide_d = jnp.concatenate([top_half, tail.astype(jnp.bfloat16)], 1)
        chosen = pick(table, head, True)
        left, right = factors(query, chosen)
        feat = (left * right * carried_ref[...]).astype(jnp.bfloat16)
        d_feat = nt(wide_d, head_state(state, den, head)) * carried_ref[...]
        dq = dq + nt((d_feat * right).astype(jnp.bfloat16), chosen[0])
        dq = dq + nt((d_feat * left).astype(jnp.bfloat16), chosen[1])
        both = tn(feat, wide_d)[:NFEAT]
        d_state = d_state + both[:, :128]
        column = jnp.sum(both[:, 128:], axis=1, keepdims=True)
        d_den = d_den + jnp.where(flane == head, column, 0.0)
        rows = []
        for b in range(2):
            top, end = b * block, (b + 1) * block
            shifted = nt(q_head[top:end], key[:end]) + 1.0
            kernel = jnp.where(masks[b], 0.5 * shifted * shifted + 0.5, 0.0).astype(jnp.bfloat16)
            pull = nt(wide_d[top:end], wide_v[:end])
            weight = jnp.where(masks[b], pull * shifted, 0.0).astype(jnp.bfloat16)
            rows.append(nn(weight, k_head[:end]))
            back_k = tn(weight, q_head[top:end])
            back_v = tn(kernel, top_half[top:end])
            for c in range(b + 1):
                dk[c] = dk[c] + back_k[c * block : (c + 1) * block]
                dv[c] = dv[c] + back_v[c * block : (c + 1) * block]
        dq = dq + jnp.concatenate(rows, 0)
    dq_ref[...] += dq
    dk_ref[...] += jnp.concatenate(dk, 0)
    dv_ref[...] = jnp.concatenate(dv, 0)
    dstate_ref[...] = d_state.astype(jnp.bfloat16)
    dden_ref[...] += d_den.astype(jnp.bfloat16)


def state_back_kernel(
    k_ref, v_ref, chosen_ref, dstate_ref, dden_ref, table_ref, dkin_ref, dvin_ref,
    dk_ref, dv_ref, hold_ref,
):
    pair = pl.program_id(0)
    table = table_ref[...]
    key = k_ref[...]
    length = key.shape[0]
    wide_v = jnp.concatenate([v_ref[...], jnp.ones((length, 128), jnp.bfloat16)], 1)

    @pl.when(pair == 0)
    def _():
        hold_ref[...] = dkin_ref[...]

    flane = lanes_of((NFEAT, 128))
    dv = dvin_ref[...]
    dk = jnp.zeros((length, WIDE), jnp.float32)
    for half in range(2):
        head = 2 * pair + half
        side = (flane >= VD) if half else (flane < VD)
        d_state = jnp.where(side, dstate_ref[...].astype(jnp.float32), 0.0)
        d_den = jnp.where(flane == head, dden_ref[...].astype(jnp.float32), 0.0)
        wide_d = padded(jnp.concatenate([d_state, d_den], 1).astype(jnp.bfloat16))
        chosen = pick(table, head, False)
        left, right = factors(key, chosen)
        feat = (left * right * chosen_ref[...]).astype(jnp.bfloat16)
        d_feat = nt(wide_v, wide_d) * chosen_ref[...]
        dk = dk + nt((d_feat * right).astype(jnp.bfloat16), chosen[0])
        dk = dk + nt((d_feat * left).astype(jnp.bfloat16), chosen[1])
        dv = dv + nn(feat, wide_d[:, :128])
    hold_ref[...] += dk
    dv_ref[...] = dv.astype(jnp.bfloat16)

    @pl.when(pair == pl.num_programs(0) - 1)
    def _():
        dk_ref[...] = hold_ref[...].astype(jnp.bfloat16)


def whole(shape):
    return pl.BlockSpec(shape, lambda i: (0,) * len(shape))


def striped(rows):
    return pl.BlockSpec((rows, 128), lambda i: (0, i))


PARAMS = pltpu.CompilerParams(
    dimension_semantics=("arbitrary",), vmem_limit_bytes=48 * 1024 * 1024
)


def call_state(key, value, chosen, table):
    length = key.shape[0]
    return pl.pallas_call(
        state_kernel,
        grid=(HEAD_PAIRS,),
        in_specs=[whole((length, WIDE)), striped(length), whole((length, 1)), whole((8, WIDE))],
        out_specs=[striped(NFEAT), whole((NFEAT, 128))],
        out_shape=[
            jax.ShapeDtypeStruct((NFEAT, FH * VD), jnp.bfloat16),
            jax.ShapeDtypeStruct((NFEAT, 128), jnp.bfloat16),
        ],
        compiler_params=PARAMS,
        name="state",
    )(key, value, chosen, table)


def mix_specs(length):
    return [
        whole((length, WIDE)), whole((length, WIDE)), striped(length), whole((length, 1)),
        whole((1, length)), whole((length, 1)), striped(NFEAT), whole((NFEAT, 128)),
        whole((8, WIDE)),
    ]


def call_mix(*args):
    length = args[0].shape[0]
    return pl.pallas_call(
        mix_kernel,
        grid=(HEAD_PAIRS,),
        in_specs=mix_specs(length),
        out_specs=[striped(length)] * 3,
        out_shape=[
            jax.ShapeDtypeStruct((length, FH * VD), jnp.bfloat16),
            jax.ShapeDtypeStruct((length, FH * VD), jnp.float32),
            jax.ShapeDtypeStruct((length, FH * VD), jnp.float32),
        ],
        compiler_params=PARAMS,
        name="mix",
    )(*args)


def call_mix_back(*args):
    length = args[0].shape[0]
    return pl.pallas_call(
        mix_back_kernel,
        grid=(HEAD_PAIRS,),
        in_specs=mix_specs(length) + [striped(length)] * 3,
        out_specs=[
            whole((length, WIDE)), whole((length, WIDE)), striped(length), striped(NFEAT),
            whole((NFEAT, 128)),
        ],
        out_shape=[
            jax.ShapeDtypeStruct((length, WIDE), jnp.float32),
            jax.ShapeDtypeStruct((length, WIDE), jnp.float32),
            jax.ShapeDtypeStruct((length, FH * VD), jnp.float32),
            jax.ShapeDtypeStruct((NFEAT, FH * VD), jnp.bfloat16),
            jax.ShapeDtypeStruct((NFEAT, 128), jnp.bfloat16),
        ],
        compiler_params=PARAMS,
        name="mix_back",
    )(*args)


def call_state_back(*args):
    length = args[0].shape[0]
    return pl.pallas_call(
        state_back_kernel,
        grid=(HEAD_PAIRS,),
        in_specs=[
            whole((length, WIDE)), striped(length), whole((length, 1)), striped(NFEAT),
            whole((NFEAT, 128)), whole((8, WIDE)), whole((length, WIDE)), striped(length),
        ],
        out_specs=[whole((length, WIDE)), striped(length)],
        out_shape=[
            jax.ShapeDtypeStruct((length, WIDE), jnp.bfloat16),
            jax.ShapeDtypeStruct((length, FH * VD), jnp.bfloat16),
        ],
        scratch_shapes=[pltpu.VMEM((length, WIDE), jnp.float32)],
        compiler_params=PARAMS,
        name="state_back",
    )(*args)


def contract_rows(left, right):
    return tn(left, right).astype(jnp.bfloat16)


def bit_of(bit):
    place = lax.axis_index("dp") * lax.axis_size("shard") + lax.axis_index("shard")
    return (place >> bit) & 1


def swap(value, bit):
    devices = lax.axis_size("dp") * lax.axis_size("shard")
    return lax.ppermute(value, BOTH, [(i, i ^ (1 << bit)) for i in range(devices)])


def bit_orders():
    bits = (lax.axis_size("dp") * lax.axis_size("shard")).bit_length() - 1
    plain = list(range(bits))
    return plain, [0] + plain[2:] + [1]


def reduce_rows(grad, order):
    rows, width = grad.shape
    size = rows // (1 << len(order))
    left = sorted(order)
    for bit in order:
        spot = left.index(bit)
        low = size << spot
        high = grad.shape[0] // (2 * low)
        cut = grad.reshape(high, 2, low, width)
        mine = bit_of(bit)
        keep = lax.dynamic_index_in_dim(cut, mine, 1, False).reshape(-1, width)
        send = lax.dynamic_index_in_dim(cut, 1 - mine, 1, False).reshape(-1, width)
        got = swap(send, bit)
        grad = (keep.astype(jnp.float32) + got.astype(jnp.float32)).astype(grad.dtype)
        left.remove(bit)
    return grad.astype(jnp.float32)


def shift(value, step):
    count = lax.axis_size("shard")
    if step > 0:
        pairs = [(i, i + step) for i in range(count - step)]
    else:
        pairs = [(i, i + step) for i in range(-step, count)]
    return lax.ppermute(value, "shard", pairs)


def norm_parts(value):
    scale = lax.rsqrt(jnp.mean(value * value, axis=-1, keepdims=True) + EPS_NORM)
    return scale, value * scale


def norm_back(scale, unit, gain, grad):
    inner = grad * gain
    return scale * (inner - unit * jnp.mean(unit * inner, axis=-1, keepdims=True)), jnp.sum(
        grad * unit, axis=0
    )


def adam_step(weight, first, second, grad, rate, decay, count):
    momentum = BETA_ONE * first + (1.0 - BETA_ONE) * grad
    variance = BETA_TWO * second + (1.0 - BETA_TWO) * grad * grad
    mean_hat = momentum / (1.0 - BETA_ONE**count)
    var_hat = variance / (1.0 - BETA_TWO**count)
    master = weight - rate * (mean_hat / (jnp.sqrt(var_hat) + ADAM_EPS) + decay * weight)
    return (master, momentum, variance)


def per_device(tokens, segments, cotangent, *state):
    masters, firsts, seconds = state[:8], state[8:16], state[16:]
    width = tokens.shape[-1]
    hidden_units = masters[4].shape[1]
    filled = -(-hidden_units // 128) * 128
    qw, vw = masters[0].shape[1], masters[2].shape[1]

    low = [w.astype(jnp.bfloat16) for w in masters]
    wide = lambda w: jnp.pad(w, ((0, 0), (0, filled - hidden_units)))
    gains_cols = jnp.pad(jnp.transpose(low[7]), ((0, 0), (0, 126)))
    pack_one = jnp.concatenate([low[0], low[1], low[2], gains_cols], axis=1)
    pack_two = jnp.concatenate([wide(low[4]), wide(low[5]), low[3], wide(low[6])], axis=1)
    all_one = lax.all_gather(pack_one, BOTH, axis=0, tiled=True)
    all_two = lax.all_gather(pack_two, BOTH, axis=0, tiled=True)
    w_qkv = all_one[:, : 2 * qw + vw]
    gains = jnp.transpose(all_one[:, 2 * qw + vw : 2 * qw + vw + 2]).astype(jnp.float32)
    gain_one, gain_two = gains[0:1], gains[1:2]
    w_lift = all_two[:, : 2 * filled]
    w_output = all_two[:, 2 * filled : 2 * filled + vw]
    w_down = all_two[:, 2 * filled + vw :]

    flat = tokens.reshape(-1, width).astype(jnp.float32)
    back = cotangent.reshape(-1, width)
    length = flat.shape[0]
    seg = segments.reshape(-1).astype(jnp.float32)
    last = seg[-1]
    table = jnp.asarray(feature_table())

    r_one, unit_one = norm_parts(flat)
    normed_one = (unit_one * gain_one).astype(jnp.bfloat16)
    qkv = nn(normed_one, w_qkv).astype(jnp.bfloat16)
    query = qkv[:, :qw] * jnp.bfloat16(FD ** (-0.5))
    key, value = qkv[:, qw : 2 * qw], qkv[:, 2 * qw :]

    chosen = (seg == last).astype(jnp.float32)[:, None]
    local_state, local_den = call_state(key, value, chosen, table)
    mark = lanes_of(local_den.shape) == 127
    local_den = jnp.where(mark, last.astype(jnp.bfloat16), local_den)
    reach = min(-(-(DOC_MAX - 1) // length), lax.axis_size("shard") - 1)
    state_in = den_in = before = None
    for step in range(1, reach + 1):
        got_state = shift(local_state, step).astype(jnp.float32)
        got_den = shift(local_den, step).astype(jnp.float32)
        if step == 1:
            state_in, den_in, before = got_state, got_den, got_den[0, 127]
        else:
            keep = (got_den[0, 127] == before).astype(jnp.float32)
            state_in, den_in = state_in + keep * got_state, den_in + keep * got_den
    state_in, den_in = state_in.astype(jnp.bfloat16), den_in.astype(jnp.bfloat16)
    carried = (seg == before).astype(jnp.float32)[:, None]
    mix_args = (
        query, key, value, seg[:, None], seg[None], carried, state_in, den_in, table,
    )
    mixed, attended, norms = call_mix(*mix_args)

    hidden = flat + nt(mixed, w_output)
    r_two, unit_two = norm_parts(hidden)
    normed_two = (unit_two * gain_two).astype(jnp.bfloat16)
    raised = nn(normed_two, w_lift)
    gate, lift = raised[:, :filled], raised[:, filled:]
    sigma = jax.nn.sigmoid(gate)
    act = (gate * sigma * lift).astype(jnp.bfloat16)
    block_out = (hidden + nt(act, w_down)).astype(jnp.bfloat16).reshape(tokens.shape)

    plain, turned = bit_orders()
    d_act = nn(back, w_down)
    d_lift = (d_act * gate * sigma).astype(jnp.bfloat16)
    d_gate = (d_act * lift * sigma * (1.0 + gate * (1.0 - sigma))).astype(jnp.bfloat16)
    d_raised = jnp.concatenate([d_gate, d_lift], axis=1)
    sum_down = reduce_rows(contract_rows(back, act), turned)
    sum_raised = reduce_rows(contract_rows(normed_two, d_raised), plain)
    d_normed_two = nt(d_raised, w_lift)
    d_hidden_norm, grad_gain_two = norm_back(r_two, unit_two, gain_two, d_normed_two)
    d_hidden = back.astype(jnp.float32) + d_hidden_norm
    dh_low = d_hidden.astype(jnp.bfloat16)
    sum_output = reduce_rows(contract_rows(dh_low, mixed), turned)
    d_mixed = nn(dh_low, w_output)

    dq, dk_part, dv_part, d_state, d_den = call_mix_back(*mix_args, attended, norms, d_mixed)
    d_den = jnp.where(mark, last.astype(jnp.bfloat16), d_den)
    state_out = den_out = after = None
    for step in range(1, reach + 1):
        got_state = shift(d_state, -step).astype(jnp.float32)
        got_den = shift(d_den, -step).astype(jnp.float32)
        if step == 1:
            state_out, den_out = got_state, got_den
        else:
            keep = (after == last).astype(jnp.float32)
            state_out, den_out = state_out + keep * got_state, den_out + keep * got_den
        after = got_den[0, 127]
    d_key, d_value = call_state_back(
        key, value, chosen, state_out.astype(jnp.bfloat16), den_out.astype(jnp.bfloat16), table,
        dk_part, dv_part,
    )
    d_query = (dq * FD ** (-0.5)).astype(jnp.bfloat16)
    d_qkv = jnp.concatenate([d_query, d_key, d_value], axis=1)
    sum_qkv = reduce_rows(contract_rows(normed_one, d_qkv), plain)
    d_normed_one = nt(d_qkv, w_qkv)
    d_flat, grad_gain_one = norm_back(r_one, unit_one, gain_one, d_normed_one)
    input_grad = (d_hidden + d_flat).reshape(tokens.shape)
    gains_grad = jnp.stack([grad_gain_one, grad_gain_two], axis=1)
    sum_gains = jnp.transpose(reduce_rows(gains_grad, plain))

    reduced = (
        sum_qkv[:, :qw],
        sum_qkv[:, qw : 2 * qw],
        sum_qkv[:, 2 * qw :],
        sum_output,
        sum_raised[:, :hidden_units],
        sum_raised[:, filled : filled + hidden_units],
        sum_down[:, :hidden_units],
        sum_gains,
    )
    squares = sum(jnp.sum(g * g) for g in (sum_qkv, sum_output, sum_raised, sum_down, sum_gains))
    grad_norm = jnp.sqrt(lax.psum(squares, BOTH))
    factor = jnp.minimum(1.0, math.sqrt(NPARAMS) / (grad_norm + 1e-06))
    base = width ** (-0.5)
    rates = (
        base, base, base, max(width // 256, 1) ** (-0.5), base, base, hidden_units ** (-0.5), 0.3,
    )
    decays = (0.1, 0.1, 0.1, 0.1, 0.1, 0.1, 0.1, 0.0)
    fresh = [
        adam_step(
            masters[i], firsts[i], seconds[i], reduced[i] * factor, rates[i], decays[i],
            float(STEP),
        )
        for i in range(8)
    ]
    return (
        block_out,
        input_grad,
        grad_norm.reshape(1),
        *[f[0] for f in fresh],
        *[f[1] for f in fresh],
        *[f[2] for f in fresh],
    )


def solution(mesh):
    return jax.shard_map(
        per_device,
        mesh=mesh,
        in_specs=(
            P("dp", "shard", None),
            P("dp", "shard"),
            P("dp", "shard", None),
            P(("dp", "shard"), None),
            P(("dp", "shard"), None),
            P(("dp", "shard"), None),
            P(("dp", "shard"), None),
            P(("dp", "shard"), None),
            P(("dp", "shard"), None),
            P(("dp", "shard"), None),
            P(None, ("dp", "shard")),
            P(("dp", "shard"), None),
            P(("dp", "shard"), None),
            P(("dp", "shard"), None),
            P(("dp", "shard"), None),
            P(("dp", "shard"), None),
            P(("dp", "shard"), None),
            P(("dp", "shard"), None),
            P(None, ("dp", "shard")),
            P(("dp", "shard"), None),
            P(("dp", "shard"), None),
            P(("dp", "shard"), None),
            P(("dp", "shard"), None),
            P(("dp", "shard"), None),
            P(("dp", "shard"), None),
            P(("dp", "shard"), None),
            P(None, ("dp", "shard")),
        ),
        out_specs=(
            P("dp", "shard", None),
            P("dp", "shard", None),
            P(),
            P(("dp", "shard"), None),
            P(("dp", "shard"), None),
            P(("dp", "shard"), None),
            P(("dp", "shard"), None),
            P(("dp", "shard"), None),
            P(("dp", "shard"), None),
            P(("dp", "shard"), None),
            P(None, ("dp", "shard")),
            P(("dp", "shard"), None),
            P(("dp", "shard"), None),
            P(("dp", "shard"), None),
            P(("dp", "shard"), None),
            P(("dp", "shard"), None),
            P(("dp", "shard"), None),
            P(("dp", "shard"), None),
            P(None, ("dp", "shard")),
            P(("dp", "shard"), None),
            P(("dp", "shard"), None),
            P(("dp", "shard"), None),
            P(("dp", "shard"), None),
            P(("dp", "shard"), None),
            P(("dp", "shard"), None),
            P(("dp", "shard"), None),
            P(None, ("dp", "shard")),
        ),
        check_vma=False,
    )
```

```python
import functools
import math

import jax
import jax.numpy as jnp
import numpy as np
from jax import lax
from jax.experimental import pallas as pl
from jax.experimental.pallas import tpu as pltpu
from jax.sharding import PartitionSpec as P

FH = 16
FD = 16
VD = 64
STEP = 10
NPARAMS = 11077632
DOC_MAX = 1024
BOTH = ("dp", "shard")

EPS_NORM = 1e-05
BETA_ONE = 0.9
BETA_TWO = 0.999
ADAM_EPS = 1e-08

HEAD_PAIRS = FH // 2
TAYLOR = [(i, j) for i in range(FD + 1) for j in range(i, FD + 1)]
NFEAT = 160
WIDE = 256


def feature_table():
    table = np.zeros((8, WIDE), np.int32)
    table[:2] = -1
    for column, (i, j) in enumerate(TAYLOR):
        table[0, column], table[1, column] = i, j
        table[2, column] = 1 if i == j and i < FD else 2
    return table


def nt(left, right):
    return lax.dot_general(
        left, right, (((1,), (1,)), ((), ())), preferred_element_type=jnp.float32
    )


def nn(left, right):
    return lax.dot_general(
        left, right, (((1,), (0,)), ((), ())), preferred_element_type=jnp.float32
    )


def tn(left, right):
    return lax.dot_general(
        left, right, (((0,), (0,)), ((), ())), preferred_element_type=jnp.float32
    )


def lanes_of(shape):
    return lax.broadcasted_iota(jnp.int32, shape, 1)


def pick(table, head, weighted):
    rows = lax.broadcasted_iota(jnp.int32, (WIDE, WIDE), 0) - FD * head
    first, second = table[0:1], table[1:2]
    size = 0.5 * table[2:3].astype(jnp.float32) if weighted else jnp.ones((1, WIDE), jnp.float32)
    inside = (rows >= 0) & (rows < FD)
    one = jnp.where(inside & (rows == first), size, 0.0).astype(jnp.bfloat16)
    two = jnp.where(inside & (rows == second), 1.0, 0.0).astype(jnp.bfloat16)
    flat_one = jnp.where(first == FD, size, 0.0)
    flat_two = jnp.where(second == FD, 1.0, 0.0)
    return one, two, flat_one, flat_two


def factors(vector, chosen):
    one, two, flat_one, flat_two = chosen
    return nn(vector, one) + flat_one, nn(vector, two) + flat_two


def padded(block):
    return jnp.concatenate([block, jnp.zeros((WIDE - block.shape[0], block.shape[1]), block.dtype)], 0)


def state_kernel(k_ref, v_ref, chosen_ref, table_ref, state_ref, den_ref):
    pair = pl.program_id(0)
    table = table_ref[...]
    key = k_ref[...]
    length = key.shape[0]
    wide_v = jnp.concatenate([v_ref[...], jnp.ones((length, 128), jnp.bfloat16)], 1)

    @pl.when(pair == 0)
    def _():
        den_ref[...] = jnp.zeros_like(den_ref)

    lane = lanes_of((NFEAT, 128))
    parts = []
    dens = jnp.zeros((NFEAT, 128), jnp.float32)
    for half in range(2):
        head = 2 * pair + half
        left, right = factors(key, pick(table, head, False))
        feat = (left * right * chosen_ref[...]).astype(jnp.bfloat16)
        both = tn(feat, wide_v)[:NFEAT]
        parts.append(both[:, :128])
        dens = dens + jnp.where(lane == head, both[:, 128:], 0.0)
    state_ref[...] = jnp.where(lane < VD, parts[0], parts[1]).astype(jnp.bfloat16)
    den_ref[...] += dens.astype(jnp.bfloat16)


def head_state(state, den, head):
    lane = lanes_of(den.shape)
    column = jnp.sum(jnp.where(lane == head, den.astype(jnp.float32), 0.0), axis=1, keepdims=True)
    column = jnp.broadcast_to(column, den.shape).astype(jnp.bfloat16)
    return padded(jnp.concatenate([state, column], 1))


def visible_block(seg_col, seg_row, top, rows, cols):
    place = lax.broadcasted_iota(jnp.int32, (rows, cols), 0) + top
    source = lax.broadcasted_iota(jnp.int32, (rows, cols), 1)
    return (source <= place) & (seg_col[top : top + rows] == seg_row[:, :cols])


def mix_kernel(
    q_ref, k_ref, v_ref, segc_ref, segr_ref, carried_ref, state_ref, den_ref, table_ref,
    low_ref, att_ref, norm_ref,
):
    pair = pl.program_id(0)
    table = table_ref[...]
    query, key = q_ref[...], k_ref[...]
    length = key.shape[0]
    block = length // 2
    wide_v = jnp.concatenate([v_ref[...], jnp.ones((length, 128), jnp.bfloat16)], 1)
    state, den = state_ref[...], den_ref[...]
    lane = lanes_of((length, WIDE)) // FD
    atts, norms = [], []
    masks = [
        visible_block(segc_ref[...], segr_ref[...], b * block, block, (b + 1) * block)
        for b in range(2)
    ]
    for half in range(2):
        head = 2 * pair + half
        q_head = jnp.where(lane == head, query, jnp.zeros_like(query))
        left, right = factors(query, pick(table, head, True))
        feat = (left * right * carried_ref[...]).astype(jnp.bfloat16)
        carried = nn(feat, head_state(state, den, head))
        sums = []
        for b in range(2):
            top, end = b * block, (b + 1) * block
            shifted = nt(q_head[top:end], key[:end]) + 1.0
            kernel = jnp.where(masks[b], 0.5 * shifted * shifted + 0.5, 0.0)
            sums.append(nn(kernel.astype(jnp.bfloat16), wide_v[:end]))
        both = jnp.concatenate(sums, 0) + carried
        atts.append(both[:, :128] / both[:, 128:])
        norms.append(both[:, 128:])
    side = lanes_of((length, 128)) < VD
    att = jnp.where(side, atts[0], atts[1])
    low_ref[...] = att.astype(jnp.bfloat16)
    att_ref[...] = att
    norm_ref[...] = jnp.where(side, norms[0], norms[1])


def mix_back_kernel(
    q_ref, k_ref, v_ref, segc_ref, segr_ref, carried_ref, state_ref, den_ref, table_ref,
    att_ref, norm_ref, dm_ref,
    dq_ref, dk_ref, dv_ref, dstate_ref, dden_ref,
):
    pair = pl.program_id(0)
    table = table_ref[...]
    query, key = q_ref[...], k_ref[...]
    length = key.shape[0]
    block = length // 2
    wide_v = jnp.concatenate([v_ref[...], jnp.ones((length, 128), jnp.bfloat16)], 1)
    state, den = state_ref[...], den_ref[...]
    lane = lanes_of((length, WIDE)) // FD
    narrow = lanes_of((length, 128))
    d_num = dm_ref[...] / norm_ref[...]
    weighted = d_num * att_ref[...]

    @pl.when(pair == 0)
    def _():
        dq_ref[...] = jnp.zeros_like(dq_ref)
        dk_ref[...] = jnp.zeros_like(dk_ref)
        dden_ref[...] = jnp.zeros_like(dden_ref)

    masks = [
        visible_block(segc_ref[...], segr_ref[...], b * block, block, (b + 1) * block)
        for b in range(2)
    ]
    flane = lanes_of((NFEAT, 128))
    d_state = jnp.zeros((NFEAT, 128), jnp.float32)
    d_den = jnp.zeros((NFEAT, 128), jnp.float32)
    dv = [jnp.zeros((block, 128), jnp.float32) for _ in range(2)]
    dk = [jnp.zeros((block, WIDE), jnp.float32) for _ in range(2)]
    dq = jnp.zeros((length, WIDE), jnp.float32)
    for half in range(2):
        head = 2 * pair + half
        side = (narrow >= VD) if half else (narrow < VD)
        q_head = jnp.where(lane == head, query, jnp.zeros_like(query))
        k_head = jnp.where(lane == head, key, jnp.zeros_like(key))
        d_bot = -jnp.sum(jnp.where(side, weighted, 0.0), axis=1, keepdims=True)
        high = d_bot.astype(jnp.bfloat16).astype(jnp.float32)
        tail = jnp.where(narrow == 0, high, jnp.where(narrow == 1, d_bot - high, 0.0))
        top_half = jnp.where(side, d_num, 0.0).astype(jnp.bfloat16)
        wide_d = jnp.concatenate([top_half, tail.astype(jnp.bfloat16)], 1)
        chosen = pick(table, head, True)
        left, right = factors(query, chosen)
        feat = (left * right * carried_ref[...]).astype(jnp.bfloat16)
        d_feat = nt(wide_d, head_state(state, den, head)) * carried_ref[...]
        dq = dq + nt((d_feat * right).astype(jnp.bfloat16), chosen[0])
        dq = dq + nt((d_feat * left).astype(jnp.bfloat16), chosen[1])
        both = tn(feat, wide_d)[:NFEAT]
        d_state = d_state + both[:, :128]
        column = jnp.sum(both[:, 128:], axis=1, keepdims=True)
        d_den = d_den + jnp.where(flane == head, column, 0.0)
        rows = []
        for b in range(2):
            top, end = b * block, (b + 1) * block
            shifted = nt(q_head[top:end], key[:end]) + 1.0
            kernel = jnp.where(masks[b], 0.5 * shifted * shifted + 0.5, 0.0).astype(jnp.bfloat16)
            pull = nt(wide_d[top:end], wide_v[:end])
            weight = jnp.where(masks[b], pull * shifted, 0.0).astype(jnp.bfloat16)
            rows.append(nn(weight, k_head[:end]))
            back_k = tn(weight, q_head[top:end])
            back_v = tn(kernel, top_half[top:end])
            for c in range(b + 1):
                dk[c] = dk[c] + back_k[c * block : (c + 1) * block]
                dv[c] = dv[c] + back_v[c * block : (c + 1) * block]
        dq = dq + jnp.concatenate(rows, 0)
    dq_ref[...] += dq
    dk_ref[...] += jnp.concatenate(dk, 0)
    dv_ref[...] = jnp.concatenate(dv, 0)
    dstate_ref[...] = d_state.astype(jnp.bfloat16)
    dden_ref[...] += d_den.astype(jnp.bfloat16)


def state_back_kernel(
    k_ref, v_ref, chosen_ref, dstate_ref, dden_ref, table_ref, dkin_ref, dvin_ref,
    dk_ref, dv_ref, hold_ref,
):
    pair = pl.program_id(0)
    table = table_ref[...]
    key = k_ref[...]
    length = key.shape[0]
    wide_v = jnp.concatenate([v_ref[...], jnp.ones((length, 128), jnp.bfloat16)], 1)

    @pl.when(pair == 0)
    def _():
        hold_ref[...] = dkin_ref[...]

    flane = lanes_of((NFEAT, 128))
    dv = dvin_ref[...]
    dk = jnp.zeros((length, WIDE), jnp.float32)
    for half in range(2):
        head = 2 * pair + half
        side = (flane >= VD) if half else (flane < VD)
        d_state = jnp.where(side, dstate_ref[...].astype(jnp.float32), 0.0)
        d_den = jnp.where(flane == head, dden_ref[...].astype(jnp.float32), 0.0)
        wide_d = padded(jnp.concatenate([d_state, d_den], 1).astype(jnp.bfloat16))
        chosen = pick(table, head, False)
        left, right = factors(key, chosen)
        feat = (left * right * chosen_ref[...]).astype(jnp.bfloat16)
        d_feat = nt(wide_v, wide_d) * chosen_ref[...]
        dk = dk + nt((d_feat * right).astype(jnp.bfloat16), chosen[0])
        dk = dk + nt((d_feat * left).astype(jnp.bfloat16), chosen[1])
        dv = dv + nn(feat, wide_d[:, :128])
    hold_ref[...] += dk
    dv_ref[...] = dv.astype(jnp.bfloat16)

    @pl.when(pair == pl.num_programs(0) - 1)
    def _():
        dk_ref[...] = hold_ref[...].astype(jnp.bfloat16)


def whole(shape):
    return pl.BlockSpec(shape, lambda i: (0,) * len(shape))


def striped(rows):
    return pl.BlockSpec((rows, 128), lambda i: (0, i))


PARAMS = pltpu.CompilerParams(
    dimension_semantics=("arbitrary",), vmem_limit_bytes=48 * 1024 * 1024
)


def call_state(key, value, chosen, table):
    length = key.shape[0]
    return pl.pallas_call(
        state_kernel,
        grid=(HEAD_PAIRS,),
        in_specs=[whole((length, WIDE)), striped(length), whole((length, 1)), whole((8, WIDE))],
        out_specs=[striped(NFEAT), whole((NFEAT, 128))],
        out_shape=[
            jax.ShapeDtypeStruct((NFEAT, FH * VD), jnp.bfloat16),
            jax.ShapeDtypeStruct((NFEAT, 128), jnp.bfloat16),
        ],
        compiler_params=PARAMS,
        name="state",
    )(key, value, chosen, table)


def mix_specs(length):
    return [
        whole((length, WIDE)), whole((length, WIDE)), striped(length), whole((length, 1)),
        whole((1, length)), whole((length, 1)), striped(NFEAT), whole((NFEAT, 128)),
        whole((8, WIDE)),
    ]


def call_mix(*args):
    length = args[0].shape[0]
    return pl.pallas_call(
        mix_kernel,
        grid=(HEAD_PAIRS,),
        in_specs=mix_specs(length),
        out_specs=[striped(length)] * 3,
        out_shape=[
            jax.ShapeDtypeStruct((length, FH * VD), jnp.bfloat16),
            jax.ShapeDtypeStruct((length, FH * VD), jnp.float32),
            jax.ShapeDtypeStruct((length, FH * VD), jnp.float32),
        ],
        compiler_params=PARAMS,
        name="mix",
    )(*args)


def call_mix_back(*args):
    length = args[0].shape[0]
    return pl.pallas_call(
        mix_back_kernel,
        grid=(HEAD_PAIRS,),
        in_specs=mix_specs(length) + [striped(length)] * 3,
        out_specs=[
            whole((length, WIDE)), whole((length, WIDE)), striped(length), striped(NFEAT),
            whole((NFEAT, 128)),
        ],
        out_shape=[
            jax.ShapeDtypeStruct((length, WIDE), jnp.float32),
            jax.ShapeDtypeStruct((length, WIDE), jnp.float32),
            jax.ShapeDtypeStruct((length, FH * VD), jnp.float32),
            jax.ShapeDtypeStruct((NFEAT, FH * VD), jnp.bfloat16),
            jax.ShapeDtypeStruct((NFEAT, 128), jnp.bfloat16),
        ],
        compiler_params=PARAMS,
        name="mix_back",
    )(*args)


def call_state_back(*args):
    length = args[0].shape[0]
    return pl.pallas_call(
        state_back_kernel,
        grid=(HEAD_PAIRS,),
        in_specs=[
            whole((length, WIDE)), striped(length), whole((length, 1)), striped(NFEAT),
            whole((NFEAT, 128)), whole((8, WIDE)), whole((length, WIDE)), striped(length),
        ],
        out_specs=[whole((length, WIDE)), striped(length)],
        out_shape=[
            jax.ShapeDtypeStruct((length, WIDE), jnp.bfloat16),
            jax.ShapeDtypeStruct((length, FH * VD), jnp.bfloat16),
        ],
        scratch_shapes=[pltpu.VMEM((length, WIDE), jnp.float32)],
        compiler_params=PARAMS,
        name="state_back",
    )(*args)


def split_kernel(low, bit_ref, left_ref, right_ref, send_ref, keep_ref, turned_ref, rows_ref):
    half = turned_ref.shape[0] // 2
    splits = half // low

    @pl.when(pl.program_id(0) == 0)
    def _():
        turned_ref[...] = jnp.transpose(left_ref[...])
        mine = bit_ref[0]
        for high in range(splits):
            for side in range(2):
                start = pl.multiple_of((2 * high + (mine if side else 1 - mine)) * low, low)
                to = side * half + high * low
                rows_ref[to : to + low] = turned_ref[pl.ds(start, low)]

    both = nn(rows_ref[...], right_ref[...]).astype(jnp.bfloat16)
    send_ref[...] = both[:half]
    keep_ref[...] = both[half:]


def call_split(left, right, mine, low):
    length, rows = left.shape
    width = right.shape[1]
    block = next(b for b in (512, 384, 256, 128) if width % b == 0)
    half = rows // 2
    kernel = functools.partial(split_kernel, low)
    return pl.pallas_call(
        kernel,
        grid_spec=pltpu.PrefetchScalarGridSpec(
            num_scalar_prefetch=1,
            grid=(width // block,),
            in_specs=[
                pl.BlockSpec((length, rows), lambda i, b: (0, 0)),
                pl.BlockSpec((length, block), lambda i, b: (0, i)),
            ],
            out_specs=[pl.BlockSpec((half, block), lambda i, b: (0, i))] * 2,
            scratch_shapes=[
                pltpu.VMEM((rows, length), jnp.bfloat16),
                pltpu.VMEM((rows, length), jnp.bfloat16),
            ],
        ),
        out_shape=[jax.ShapeDtypeStruct((half, width), jnp.bfloat16)] * 2,
        compiler_params=PARAMS,
        name="split",
    )(mine, left, right)


def contract_rows(left, right):
    return tn(left, right).astype(jnp.bfloat16)


def bit_of(bit):
    place = lax.axis_index("dp") * lax.axis_size("shard") + lax.axis_index("shard")
    return (place >> bit) & 1


def swap(value, bit):
    devices = lax.axis_size("dp") * lax.axis_size("shard")
    return lax.ppermute(value, BOTH, [(i, i ^ (1 << bit)) for i in range(devices)])


def bit_orders():
    bits = (lax.axis_size("dp") * lax.axis_size("shard")).bit_length() - 1
    rest = list(range(1, bits))
    return [[0] + rest, [0] + rest[1:2] + rest[:1] + rest[2:], [0] + rest[2:3] + rest[1::-1] + rest[3:]]


def add_low(one, two):
    return (one.astype(jnp.float32) + two.astype(jnp.float32)).astype(one.dtype)


def split_rows(left, right):
    rows = left.shape[1]
    low = rows // (lax.axis_size("dp") * lax.axis_size("shard"))
    mine = bit_of(0)
    if low % 16 == 0 and right.shape[1] % 128 == 0:
        return call_split(left, right, mine.reshape(1), low)
    return halve(contract_rows(left, right), mine, low)


def halve(grad, mine, low):
    width = grad.shape[1]
    cut = grad.reshape(-1, 2, low, width)
    keep = lax.dynamic_index_in_dim(cut, mine, 1, False).reshape(-1, width)
    send = lax.dynamic_index_in_dim(cut, 1 - mine, 1, False).reshape(-1, width)
    return send, keep


def reduce_rows(send, keep, order):
    size = 2 * send.shape[0] // (1 << len(order))
    left = sorted(order)
    grad = None
    for bit in order:
        if grad is not None:
            send, keep = halve(grad, bit_of(bit), size << left.index(bit))
        grad = add_low(keep, swap(send, bit))
        left.remove(bit)
    return grad.astype(jnp.float32)


def total(value):
    devices = lax.axis_size("dp") * lax.axis_size("shard")
    value = jnp.full((8, 128), value, jnp.float32)
    for bit in range(devices.bit_length() - 1):
        value = value + swap(value, bit)
    return value[0, 0]


def shift(value, step):
    count = lax.axis_size("shard")
    if step > 0:
        pairs = [(i, i + step) for i in range(count - step)]
    else:
        pairs = [(i, i + step) for i in range(-step, count)]
    return lax.ppermute(value, "shard", pairs)


def norm_parts(value):
    scale = lax.rsqrt(jnp.mean(value * value, axis=-1, keepdims=True) + EPS_NORM)
    return scale, value * scale


def norm_back(scale, unit, gain, grad):
    inner = grad * gain
    return scale * (inner - unit * jnp.mean(unit * inner, axis=-1, keepdims=True)), jnp.sum(
        grad * unit, axis=0
    )


def adam_step(weight, first, second, grad, rate, decay, count):
    momentum = BETA_ONE * first + (1.0 - BETA_ONE) * grad
    variance = BETA_TWO * second + (1.0 - BETA_TWO) * grad * grad
    mean_hat = momentum / (1.0 - BETA_ONE**count)
    var_hat = variance / (1.0 - BETA_TWO**count)
    master = weight - rate * (mean_hat / (jnp.sqrt(var_hat) + ADAM_EPS) + decay * weight)
    return (master, momentum, variance)


def per_device(tokens, segments, cotangent, *state):
    masters, firsts, seconds = state[:8], state[8:16], state[16:]
    width = tokens.shape[-1]
    hidden_units = masters[4].shape[1]
    filled = -(-hidden_units // 128) * 128
    qw, vw = masters[0].shape[1], masters[2].shape[1]

    low = [w.astype(jnp.bfloat16) for w in masters]
    wide = lambda w: jnp.pad(w, ((0, 0), (0, filled - hidden_units)))
    gains_cols = jnp.pad(jnp.transpose(low[7]), ((0, 0), (0, 126)))
    pack_one = jnp.concatenate([low[0], low[1], low[2], gains_cols], axis=1)
    pack_two = jnp.concatenate([wide(low[4]), wide(low[5]), low[3]], axis=1)
    all_one = lax.all_gather(pack_one, BOTH, axis=0, tiled=True)
    all_two = lax.all_gather(pack_two, BOTH, axis=0, tiled=True)
    w_down = lax.all_gather(wide(low[6]), BOTH, axis=0, tiled=True)
    w_qkv = all_one[:, : 2 * qw + vw]
    gains = jnp.transpose(all_one[:, 2 * qw + vw : 2 * qw + vw + 2]).astype(jnp.float32)
    gain_one, gain_two = gains[0:1], gains[1:2]
    w_lift = all_two[:, : 2 * filled]
    w_output = all_two[:, 2 * filled :]

    flat = tokens.reshape(-1, width).astype(jnp.float32)
    back = cotangent.reshape(-1, width)
    length = flat.shape[0]
    seg = segments.reshape(-1).astype(jnp.float32)
    last = seg[-1]
    table = jnp.asarray(feature_table())

    r_one, unit_one = norm_parts(flat)
    normed_one = (unit_one * gain_one).astype(jnp.bfloat16)
    qkv = nn(normed_one, w_qkv).astype(jnp.bfloat16)
    query = qkv[:, :qw] * jnp.bfloat16(FD ** (-0.5))
    key, value = qkv[:, qw : 2 * qw], qkv[:, 2 * qw :]

    chosen = (seg == last).astype(jnp.float32)[:, None]
    local_state, local_den = call_state(key, value, chosen, table)
    mark = lanes_of(local_den.shape) == 127
    local_den = jnp.where(mark, last.astype(jnp.bfloat16), local_den)
    reach = min(-(-(DOC_MAX - 1) // length), lax.axis_size("shard") - 1)
    state_in = den_in = before = None
    for step in range(1, reach + 1):
        got_state = shift(local_state, step).astype(jnp.float32)
        got_den = shift(local_den, step).astype(jnp.float32)
        if step == 1:
            state_in, den_in, before = got_state, got_den, got_den[0, 127]
        else:
            keep = (got_den[0, 127] == before).astype(jnp.float32)
            state_in, den_in = state_in + keep * got_state, den_in + keep * got_den
    state_in, den_in = state_in.astype(jnp.bfloat16), den_in.astype(jnp.bfloat16)
    carried = (seg == before).astype(jnp.float32)[:, None]
    mix_args = (
        query, key, value, seg[:, None], seg[None], carried, state_in, den_in, table,
    )
    mixed, attended, norms = call_mix(*mix_args)

    hidden = flat + nt(mixed, w_output)
    r_two, unit_two = norm_parts(hidden)
    normed_two = (unit_two * gain_two).astype(jnp.bfloat16)
    raised = nn(normed_two, w_lift)
    gate, lift = raised[:, :filled], raised[:, filled:]
    sigma = jax.nn.sigmoid(gate)
    act = (gate * sigma * lift).astype(jnp.bfloat16)
    block_out = (hidden + nt(act, w_down)).astype(jnp.bfloat16).reshape(tokens.shape)

    along_x, along_y, along_z = bit_orders()
    d_act = nn(back, w_down)
    d_lift = (d_act * gate * sigma).astype(jnp.bfloat16)
    d_gate = (d_act * lift * sigma * (1.0 + gate * (1.0 - sigma))).astype(jnp.bfloat16)
    cut_down = split_rows(back, act)
    cut_gate = split_rows(normed_two, d_gate)
    cut_up = split_rows(normed_two, d_lift)
    d_raised = jnp.concatenate([d_gate, d_lift], axis=1)
    d_raised, cut_down, cut_gate, cut_up = lax.optimization_barrier(
        (d_raised, cut_down, cut_gate, cut_up)
    )
    sum_down = reduce_rows(*cut_down, along_z)
    sum_gate = reduce_rows(*cut_gate, along_x)
    sum_up = reduce_rows(*cut_up, along_y)
    d_normed_two = nt(d_raised, w_lift)
    d_hidden_norm, grad_gain_two = norm_back(r_two, unit_two, gain_two, d_normed_two)
    d_hidden = back.astype(jnp.float32) + d_hidden_norm
    dh_low = d_hidden.astype(jnp.bfloat16)
    dh_low, cut_output = lax.optimization_barrier((dh_low, split_rows(dh_low, mixed)))
    sum_output = reduce_rows(*cut_output, along_x)
    d_mixed = nn(dh_low, w_output)

    dq, dk_part, dv_part, d_state, d_den = call_mix_back(*mix_args, attended, norms, d_mixed)
    d_den = jnp.where(mark, last.astype(jnp.bfloat16), d_den)
    state_out = den_out = after = None
    for step in range(1, reach + 1):
        got_state = shift(d_state, -step).astype(jnp.float32)
        got_den = shift(d_den, -step).astype(jnp.float32)
        if step == 1:
            state_out, den_out = got_state, got_den
        else:
            keep = (after == last).astype(jnp.float32)
            state_out, den_out = state_out + keep * got_state, den_out + keep * got_den
        after = got_den[0, 127]
    d_key, d_value = call_state_back(
        key, value, chosen, state_out.astype(jnp.bfloat16), den_out.astype(jnp.bfloat16), table,
        dk_part, dv_part,
    )
    d_query = (dq * FD ** (-0.5)).astype(jnp.bfloat16)
    d_qk = jnp.concatenate([d_query, d_key], axis=1)
    cut_value = split_rows(normed_one, d_value)
    cut_qk = split_rows(normed_one, d_qk)
    d_qkv = jnp.concatenate([d_qk, d_value], axis=1)
    d_qkv, cut_value, cut_qk = lax.optimization_barrier((d_qkv, cut_value, cut_qk))
    sum_value = reduce_rows(*cut_value, along_x)
    sum_qk = reduce_rows(*cut_qk, along_y)
    d_normed_one = nt(d_qkv, w_qkv)
    d_flat, grad_gain_one = norm_back(r_one, unit_one, gain_one, d_normed_one)
    input_grad = (d_hidden + d_flat).reshape(tokens.shape)
    gains_grad = jnp.stack([grad_gain_one, grad_gain_two], axis=1)
    size = width // (lax.axis_size("dp") * lax.axis_size("shard"))
    sum_gains = jnp.transpose(reduce_rows(*halve(gains_grad, bit_of(0), size), along_z))

    reduced = (
        sum_qk[:, :qw],
        sum_qk[:, qw:],
        sum_value,
        sum_output,
        sum_gate[:, :hidden_units],
        sum_up[:, :hidden_units],
        sum_down[:, :hidden_units],
        sum_gains,
    )
    squares = sum(jnp.sum(g * g) for g in reduced)
    grad_norm = jnp.sqrt(total(squares))
    factor = jnp.minimum(1.0, math.sqrt(NPARAMS) / (grad_norm + 1e-06))
    base = width ** (-0.5)
    rates = (
        base, base, base, max(width // 256, 1) ** (-0.5), base, base, hidden_units ** (-0.5), 0.3,
    )
    decays = (0.1, 0.1, 0.1, 0.1, 0.1, 0.1, 0.1, 0.0)
    fresh = [
        adam_step(
            masters[i], firsts[i], seconds[i], reduced[i] * factor, rates[i], decays[i],
            float(STEP),
        )
        for i in range(8)
    ]
    return (
        block_out,
        input_grad,
        grad_norm.reshape(1),
        *[f[0] for f in fresh],
        *[f[1] for f in fresh],
        *[f[2] for f in fresh],
    )


def solution(mesh):
    return jax.shard_map(
        per_device,
        mesh=mesh,
        in_specs=(
            P("dp", "shard", None),
            P("dp", "shard"),
            P("dp", "shard", None),
            P(("dp", "shard"), None),
            P(("dp", "shard"), None),
            P(("dp", "shard"), None),
            P(("dp", "shard"), None),
            P(("dp", "shard"), None),
            P(("dp", "shard"), None),
            P(("dp", "shard"), None),
            P(None, ("dp", "shard")),
            P(("dp", "shard"), None),
            P(("dp", "shard"), None),
            P(("dp", "shard"), None),
            P(("dp", "shard"), None),
            P(("dp", "shard"), None),
            P(("dp", "shard"), None),
            P(("dp", "shard"), None),
            P(None, ("dp", "shard")),
            P(("dp", "shard"), None),
            P(("dp", "shard"), None),
            P(("dp", "shard"), None),
            P(("dp", "shard"), None),
            P(("dp", "shard"), None),
            P(("dp", "shard"), None),
            P(("dp", "shard"), None),
            P(None, ("dp", "shard")),
        ),
        out_specs=(
            P("dp", "shard", None),
            P("dp", "shard", None),
            P(),
            P(("dp", "shard"), None),
            P(("dp", "shard"), None),
            P(("dp", "shard"), None),
            P(("dp", "shard"), None),
            P(("dp", "shard"), None),
            P(("dp", "shard"), None),
            P(("dp", "shard"), None),
            P(None, ("dp", "shard")),
            P(("dp", "shard"), None),
            P(("dp", "shard"), None),
            P(("dp", "shard"), None),
            P(("dp", "shard"), None),
            P(("dp", "shard"), None),
            P(("dp", "shard"), None),
            P(("dp", "shard"), None),
            P(None, ("dp", "shard")),
            P(("dp", "shard"), None),
            P(("dp", "shard"), None),
            P(("dp", "shard"), None),
            P(("dp", "shard"), None),
            P(("dp", "shard"), None),
            P(("dp", "shard"), None),
            P(("dp", "shard"), None),
            P(None, ("dp", "shard")),
        ),
        check_vma=False,
    )
```
